32 devices in a mesh: dp: 8 (over z, y), fsdp: 4 (over x, core).
Axes of the slice: x: 2, y: 2, z: 4, core: 2. Of those that a mesh axis runs over, the one named last changes fastest.
Arguments:
- tiles: bfloat16 [768, 4096], P('fsdp', 'dp'), may hold values from -6 to 6
- kernel: bfloat16 [49, 768], P(None, 'fsdp'), may hold values from -0.875 to 0.875
- norm_gain: bfloat16 [768], P('fsdp'), may hold values from 0.099609375 to 1.8984375
- w_up: bfloat16 [768, 1536], P('dp', 'fsdp'), may hold values from -0.21875 to 0.21875
- w_down: bfloat16 [768, 1536], P('dp', 'fsdp'), may hold values from -0.15625 to 0.15625
- layer_scale: bfloat16 [768], P('fsdp'), may hold values from 0.5 to 2
- neighbors: int32 [64, 4, 2], P('dp'), may hold values from -1 to 63, as said below
- shifts: int32 [64, 4, 2], P('dp'), may hold values from -8 to 7, as said below
- halo_widths: int32 [64, 4], P('dp'), may hold values from 1 to 3
- land: int32 [64, 8, 8], P('dp'), may hold values 0 or 1
- cotangent: bfloat16 [768, 4096], P('fsdp', 'dp'), may hold values from -6 to 6
Outputs:
- block_out: bfloat16 [768, 4096], P('fsdp', 'dp')
- tile_grad: bfloat16 [768, 4096], P('fsdp', 'dp')
- up_grad: float32 [768, 1536], P('dp', 'fsdp')
- down_grad: float32 [768, 1536], P('dp', 'fsdp')
The draws below stay inside these ranges and needn't reach their ends.
Inputs may be any that keep to these rules, and one draw needn't show every extreme that they name: `neighbors`: faces are north, south, west, east. Tile t is held by index t // 8 of dp. A named north or south neighbour is held by the same index of dp as the tile, a west one by the index before, an east one by the index after. Adjacency is symmetric: a cell taken from a neighbour's edge belongs to the tile that takes the facing cell of it. Entry 0 of a face holds shifts 0 to 7, entry 1 shifts -8 to -1; an entry that names no tile has shift 0, and north and south shifts are 0.
All inputs are finite; a program needn't handle non-finite values. No bound on the sum of `land` on one device may be relied on, other than what follows from the above.
Results may differ from the reference program's by a relative error of at most 0.0095.
Values may be sent and summed in bfloat16 or wider, within the bound.
No kernel may reach another device: no remote copies, remote signals or barrier semaphores. Data moves between devices by JAX's collectives and lax.ppermute only.
A program may use at most 64 MiB of HBM per device.

```python
import math
import jax
import jax.numpy as jnp
from jax import lax

WIDTH = 768
HIDDEN_SIZE = 1536
KSIZE = 7
SIDE = 8
TILE_DEV = 8
TILES = 64
N_FSDP = 4


def tile_layout(key):
    columns = TILES // TILE_DEV
    scores = jax.random.randint(jax.random.fold_in(key, 11), (columns, TILE_DEV), 0, 1 << 20) * TILE_DEV + jnp.arange(TILE_DEV, dtype=jnp.int32)[None, :]
    row_of_slot = jnp.argsort(scores, axis=1).astype(jnp.int32)
    slot_of_row = jnp.argsort(row_of_slot, axis=1).astype(jnp.int32)
    base_row = jax.random.randint(jax.random.fold_in(key, 7), (columns,), 0, SIDE).astype(jnp.int32)
    tile_index = jnp.arange(TILES, dtype=jnp.int32)
    column = tile_index // TILE_DEV
    tile_row = row_of_slot[column, tile_index % TILE_DEV]
    none_tile = jnp.full((TILES,), -1, jnp.int32)
    zero_shift = jnp.zeros((TILES,), jnp.int32)
    owner_list = []
    shift_list = []
    for step_row in (-1, 1):
        other_row = tile_row + step_row
        inside = (other_row >= 0) & (other_row < TILE_DEV)
        named = column * TILE_DEV + slot_of_row[column, jnp.clip(other_row, 0, TILE_DEV - 1)]
        owner_list.append(jnp.stack([jnp.where(inside, named, -1), none_tile], axis=1))
        shift_list.append(jnp.stack([zero_shift, zero_shift], axis=1))
    for step_col in (-1, 1):
        other_col = column + step_col
        col_inside = (other_col >= 0) & (other_col < columns)
        safe_col = jnp.clip(other_col, 0, columns - 1)
        start_row = base_row[column] - base_row[safe_col] + SIDE * tile_row
        first_row = start_row // SIDE
        first_shift = start_row - SIDE * first_row
        entries = []
        moves = []
        for which_entry in range(2):
            near_row = first_row + which_entry
            inside = col_inside & (near_row >= 0) & (near_row < TILE_DEV)
            named = safe_col * TILE_DEV + slot_of_row[safe_col, jnp.clip(near_row, 0, TILE_DEV - 1)]
            entries.append(jnp.where(inside, named, -1))
            moves.append(jnp.where(inside, first_shift - SIDE * which_entry, 0))
        owner_list.append(jnp.stack(entries, axis=1))
        shift_list.append(jnp.stack(moves, axis=1))
    return (jnp.stack(owner_list, axis=1).astype(jnp.int32), jnp.stack(shift_list, axis=1).astype(jnp.int32))


def draw_neighbors(key, part):
    return tile_layout(key)[0]


def draw_shifts(key, part):
    return tile_layout(key)[1]


def touch_ends(drawn, own_key, smallest, largest):
    longest = drawn.shape.index(max(drawn.shape))
    spots = []
    for shift in (0, 1):
        where = [jax.random.randint(jax.random.fold_in(own_key, axis), (), 0, length) for axis, length in enumerate(drawn.shape)]
        where[longest] = (where[longest] + shift) % drawn.shape[longest]
        spots.append(tuple(where))
    return drawn.at[spots[0]].set(smallest).at[spots[1]].set(largest)


def block_levels(key, shape, pieces, smallest, top_value):
    def one(axis_at, shards_of):
        heights = jax.random.uniform(jax.random.fold_in(jax.random.fold_in(key, 6), axis_at), (shards_of,), jnp.float32, smallest / len(pieces), top_value / len(pieces))
        return jnp.repeat(jnp.exp(heights), shape[axis_at] // shards_of).reshape((-1,) + (1,) * (len(shape) - axis_at - 1))

    loudness = one(*pieces[0])
    for cut in pieces[1:]:
        loudness = loudness * one(*cut)
    return loudness


def gaussian(own_key, dims, deviation, limit, shards=(), held_as=jnp.bfloat16):
    values = jax.random.normal(own_key, dims, jnp.float32) * deviation
    if len(shards) > 0:
        values = block_levels(own_key, dims, shards, -0.22, 0.18) * values
    return jnp.clip(values, min=-limit, max=limit).astype(held_as)


def setup_inputs(seed: int = 0) -> dict:
    streams_of = jax.random.split(jax.random.key(seed), 12)
    tiles = gaussian(streams_of[0], (WIDTH, TILES * SIDE * SIDE), 1.0, 6.0, ((0, 4), (1, 8)))
    kernel = gaussian(streams_of[1], (KSIZE * KSIZE, WIDTH), (KSIZE * KSIZE) ** -0.5, 0.875, ((1, 4),))
    norm_gain = jnp.clip(1.0 + 0.18 * jax.random.normal(streams_of[2], (WIDTH,), jnp.float32), 0.099609375, 1.8984375).astype(jnp.bfloat16)
    w_up = gaussian(streams_of[3], (WIDTH, HIDDEN_SIZE), WIDTH ** -0.5, 0.21875, ((0, 8), (1, 4)))
    w_down = gaussian(streams_of[4], (WIDTH, HIDDEN_SIZE), HIDDEN_SIZE ** -0.5, 0.15625, ((0, 8), (1, 4)))
    layer_scale = jnp.clip(jnp.exp(math.log(2.0) - 1.3862944 * jax.random.uniform(streams_of[5], (WIDTH,), jnp.float32) ** block_levels(streams_of[5], (WIDTH,), ((0, 4),), -0.2, 0.2)), 0.5, 2.0).astype(jnp.bfloat16)
    neighbors = draw_neighbors(jax.random.fold_in(streams_of[11], 71), 0)
    shifts = draw_shifts(jax.random.fold_in(streams_of[11], 71), 0)
    halo_widths = touch_ends(jax.random.randint(streams_of[8], (TILES, 4), 1, 4), jax.random.fold_in(streams_of[8], 1), 1, 3).astype(jnp.int32)
    land = touch_ends((jax.random.randint(streams_of[9], (TILES, SIDE, SIDE), 0, 4) < 3).astype(jnp.int32), jax.random.fold_in(streams_of[9], 1), 0, 1)
    cotangent = gaussian(streams_of[10], (WIDTH, TILES * SIDE * SIDE), 1.0, 6.0, ((0, 4), (1, 8)))
    return {"tiles": tiles, "kernel": kernel, "norm_gain": norm_gain, "w_up": w_up, "w_down": w_down, "layer_scale": layer_scale, "neighbors": neighbors, "shifts": shifts, "halo_widths": halo_widths, "land": land, "cotangent": cotangent}


root_half = 1.0 / math.sqrt(2.0)
root_tau = 1.0 / math.sqrt(2.0 * math.pi)

def gelu_value(hidden):
    return 0.5 * hidden * (1.0 + jax.scipy.special.erf(hidden * root_half))

def gelu_slope(hidden):
    return 0.5 * (1.0 + jax.scipy.special.erf(hidden * root_half)) + hidden * jnp.exp(-0.5 * hidden * hidden) * root_tau

def depth_keep(widths_face, far_first):
    layer_index = jnp.arange(3, dtype=jnp.int32)
    if far_first:
        depth_value = 3 - layer_index
    else:
        depth_value = layer_index + 1
    return depth_value[None, :] <= widths_face[:, None]

def face_sources(tiles):
    side_len = tiles.shape[1]
    return (jnp.transpose(tiles[:, side_len - 3:], (0, 2, 1, 3)), jnp.transpose(tiles[:, :3], (0, 2, 1, 3)), tiles[:, :, side_len - 3:], tiles[:, :, :3])

def assemble(tiles, halos):
    tile_count = tiles.shape[0]
    channels = tiles.shape[3]
    corner = jnp.zeros((tile_count, 3, 3, channels), tiles.dtype)
    upper = jnp.concatenate([corner, jnp.transpose(halos[0], (0, 2, 1, 3)), corner], axis=2)
    lower = jnp.concatenate([corner, jnp.transpose(halos[1], (0, 2, 1, 3)), corner], axis=2)
    middle = jnp.concatenate([halos[2], tiles, halos[3]], axis=2)
    return jnp.concatenate([upper, middle, lower], axis=1)

def depthwise(padded, kernel):
    side_len = padded.shape[1] - 6
    taps = kernel.astype(jnp.float32)
    summed = jnp.zeros((padded.shape[0], side_len, side_len, padded.shape[3]), jnp.float32)
    for row_tap in range(7):
        for col_tap in range(7):
            window = padded[:, row_tap:row_tap + side_len, col_tap:col_tap + side_len, :].astype(jnp.float32)
            summed = summed + window * taps[row_tap * 7 + col_tap]
    return summed

def depthwise_back(grad_conv, kernel):
    side_len = grad_conv.shape[1]
    taps = kernel.astype(jnp.float32)
    spread = jnp.pad(grad_conv.astype(jnp.float32), ((0, 0), (6, 6), (6, 6), (0, 0)))
    summed = jnp.zeros((grad_conv.shape[0], side_len + 6, side_len + 6, grad_conv.shape[3]), jnp.float32)
    for row_tap in range(7):
        for col_tap in range(7):
            window = spread[:, 6 - row_tap:12 - row_tap + side_len, 6 - col_tap:12 - col_tap + side_len, :]
            summed = summed + window * taps[row_tap * 7 + col_tap]
    return summed

def pick_halo(source, neighbor_ids, shift_values):
    side_len = source.shape[1]
    position = jnp.arange(side_len, dtype=jnp.int32)
    summed = jnp.zeros(source.shape, jnp.float32)
    for which_entry in range(2):
        owner_tile = neighbor_ids[:, which_entry]
        along_edge = position[None, :] + shift_values[:, which_entry][:, None]
        is_valid = (owner_tile[:, None] >= 0) & (along_edge >= 0) & (along_edge < side_len)
        gathered = source[jnp.maximum(owner_tile, 0)]
        picked = jnp.take_along_axis(gathered, jnp.clip(along_edge, 0, side_len - 1)[:, :, None, None], axis=1)
        summed = summed + jnp.where(is_valid[:, :, None, None], picked.astype(jnp.float32), 0.0)
    return summed

def return_halo(grad_face, neighbor_ids, shift_values):
    side_len = grad_face.shape[1]
    position = jnp.arange(side_len, dtype=jnp.int32)
    summed = jnp.zeros(grad_face.shape, jnp.float32)
    for which_entry in range(2):
        owner_tile = neighbor_ids[:, which_entry]
        along_edge = position[None, :] + shift_values[:, which_entry][:, None]
        is_valid = (owner_tile[:, None] >= 0) & (along_edge >= 0) & (along_edge < side_len)
        moving = jnp.where(is_valid[:, :, None, None], grad_face, 0.0)
        summed = summed.at[jnp.maximum(owner_tile, 0)[:, None], jnp.clip(along_edge, 0, side_len - 1)].add(moving)
    return summed

def reference(tiles, kernel, norm_gain, w_up, w_down, layer_scale, neighbors, shifts, halo_widths, land, cotangent):
    channels = tiles.shape[0]
    tile_count, side_len = (land.shape[0], land.shape[1])
    tiles_grid = jnp.transpose(tiles.reshape(channels, tile_count, side_len, side_len), (1, 2, 3, 0))
    cotangent_grid = jnp.transpose(cotangent.reshape(channels, tile_count, side_len, side_len), (1, 2, 3, 0))
    row_count = tile_count * side_len * side_len
    sources = face_sources(tiles_grid)
    halos = []
    masks = []
    for face_index in range(4):
        keep_mask = depth_keep(halo_widths[:, face_index], face_index in (0, 2))[:, None, :, None]
        masks.append(keep_mask)
        picked = pick_halo(sources[face_index], neighbors[:, face_index], shifts[:, face_index])
        halos.append(jnp.where(keep_mask, picked, 0.0).astype(jnp.bfloat16))
    conv = depthwise(assemble(tiles_grid, halos), kernel)
    conv_rows = conv.reshape(row_count, channels).astype(jnp.bfloat16)
    values = lax.optimization_barrier(conv_rows).astype(jnp.float32)
    row_mean = lax.optimization_barrier(jnp.sum(values, axis=1)) / channels
    row_square = lax.optimization_barrier(jnp.sum(values * values, axis=1)) / channels
    inv_scale = lax.rsqrt(row_square - row_mean * row_mean + 1e-06)
    centered = (values - row_mean[:, None]) * inv_scale[:, None]
    gain_f = norm_gain.astype(jnp.float32)
    normed = (centered * gain_f).astype(jnp.bfloat16)
    pre_act = jnp.dot(normed, w_up, preferred_element_type=jnp.float32)
    hidden = gelu_value(pre_act).astype(jnp.bfloat16)
    block_size = w_up.shape[1] // N_FSDP
    mixed = jnp.zeros((row_count, channels), jnp.float32)
    for block_index in range(N_FSDP):
        lower_edge = block_index * block_size
        partial_out = jnp.dot(hidden[:, lower_edge:lower_edge + block_size], w_down[:, lower_edge:lower_edge + block_size].T, preferred_element_type=jnp.float32)
        mixed = mixed + lax.optimization_barrier(partial_out.astype(jnp.bfloat16)).astype(jnp.float32)
    scale_f = layer_scale.astype(jnp.float32)
    block_out = (tiles_grid.reshape(row_count, channels).astype(jnp.float32) + scale_f * mixed).astype(jnp.bfloat16).reshape(tiles_grid.shape)
    grad_out = cotangent_grid * land[:, :, :, None].astype(jnp.bfloat16)
    grad_mixed = (scale_f * grad_out.reshape(row_count, channels).astype(jnp.float32)).astype(jnp.bfloat16)
    down_grad = jnp.dot(grad_mixed.T, hidden, preferred_element_type=jnp.float32)
    grad_hidden = jnp.dot(grad_mixed, w_down, preferred_element_type=jnp.float32)
    grad_pre = (grad_hidden * gelu_slope(pre_act)).astype(jnp.bfloat16)
    up_grad = jnp.dot(normed.T, grad_pre, preferred_element_type=jnp.float32)
    grad_normed = jnp.zeros((row_count, channels), jnp.float32)
    for block_index in range(N_FSDP):
        lower_edge = block_index * block_size
        partial_grad = jnp.dot(grad_pre[:, lower_edge:lower_edge + block_size], w_up[:, lower_edge:lower_edge + block_size].T, preferred_element_type=jnp.float32)
        grad_normed = grad_normed + lax.optimization_barrier(partial_grad.astype(jnp.bfloat16)).astype(jnp.float32)
    grad_centered = grad_normed * gain_f
    first_mean = lax.optimization_barrier(jnp.sum(grad_centered, axis=1)) / channels
    second_mean = lax.optimization_barrier(jnp.sum(grad_centered * centered, axis=1)) / channels
    grad_conv = (inv_scale[:, None] * (grad_centered - first_mean[:, None] - centered * second_mean[:, None])).astype(jnp.bfloat16)
    grad_pad = depthwise_back(grad_conv.reshape(conv.shape), kernel)
    inner = slice(3, 3 + side_len)
    tile_grad = grad_out.astype(jnp.float32) + grad_pad[:, inner, inner]
    edge_north = return_halo(jnp.where(masks[0], jnp.transpose(grad_pad[:, 0:3, inner], (0, 2, 1, 3)), 0.0), neighbors[:, 0], shifts[:, 0])
    tile_grad = tile_grad + jnp.pad(jnp.transpose(edge_north, (0, 2, 1, 3)), ((0, 0), (side_len - 3, 0), (0, 0), (0, 0)))
    edge_south = return_halo(jnp.where(masks[1], jnp.transpose(grad_pad[:, side_len + 3:, inner], (0, 2, 1, 3)), 0.0), neighbors[:, 1], shifts[:, 1])
    tile_grad = tile_grad + jnp.pad(jnp.transpose(edge_south, (0, 2, 1, 3)), ((0, 0), (0, side_len - 3), (0, 0), (0, 0)))
    edge_west = return_halo(jnp.where(masks[2], grad_pad[:, inner, 0:3], 0.0), neighbors[:, 2], shifts[:, 2])
    tile_grad = tile_grad + jnp.pad(edge_west, ((0, 0), (0, 0), (side_len - 3, 0), (0, 0)))
    edge_east = return_halo(jnp.where(masks[3], grad_pad[:, inner, side_len + 3:], 0.0), neighbors[:, 3], shifts[:, 3])
    tile_grad = tile_grad + jnp.pad(edge_east, ((0, 0), (0, 0), (0, side_len - 3), (0, 0)))
    block_flat = jnp.transpose(block_out, (3, 0, 1, 2)).reshape(channels, row_count)
    grad_flat = jnp.transpose(tile_grad.astype(jnp.bfloat16), (3, 0, 1, 2)).reshape(channels, row_count)
    return (block_flat, grad_flat, up_grad, down_grad)
```

```python
import math

import jax
import jax.numpy as jnp
from jax import lax
from jax.experimental import pallas as pl
from jax.experimental.pallas import tpu as pltpu
from jax.sharding import PartitionSpec as P

root_half = 1.0 / math.sqrt(2.0)
root_tau = 1.0 / math.sqrt(2.0 * math.pi)
LAYERS = 3
KSIZE = 7
F32 = jnp.float32
BF16 = jnp.bfloat16

ROWS_LANES = (((1,), (1,)), ((), ()))
ROWS_ROWS = (((0,), (0,)), ((), ()))


def dot(a, b, dims):
    return lax.dot_general(a, b, dims, preferred_element_type=F32)


def gelu_value(hidden):
    return 0.5 * hidden * (1.0 + jax.scipy.special.erf(hidden * root_half))


def gelu_slope(hidden):
    return (
        0.5 * (1.0 + jax.scipy.special.erf(hidden * root_half))
        + hidden * jnp.exp(-0.5 * hidden * hidden) * root_tau
    )


def one_hot(target, width):
    groups, tile_count, _ = target.shape
    col = lax.broadcasted_iota(jnp.int32, (groups, tile_count, width), 2)
    hit = jnp.where(col == target, 1.0, 0.0)
    return hit.reshape(groups * tile_count, width)


def cell_order(side, tile_count):
    cells = side * side
    shape = (cells, tile_count, cells * tile_count)
    target = lax.broadcasted_iota(jnp.int32, shape, 1) * cells + lax.broadcasted_iota(
        jnp.int32, shape, 0
    )
    return one_hot(target, shape[2]).astype(BF16)


def edge_order(side, tile_count, first):
    cells = side * side
    width = cells * tile_count
    parts = []
    for layer in range(LAYERS):
        shape = (side, tile_count, width)
        target = (
            lax.broadcasted_iota(jnp.int32, shape, 1) * cells
            + lax.broadcasted_iota(jnp.int32, shape, 0) * side
            + (first + layer)
        )
        parts.append(one_hot(target, width))
    return jnp.concatenate(parts, axis=0).astype(BF16)


def by_tile(table, tile_count, width, pick):
    row = lax.broadcasted_iota(jnp.int32, (tile_count, width), 0)
    out = jnp.zeros((tile_count, width), jnp.int32)
    for tile in range(tile_count):
        out = jnp.where(row == tile, pick(table, tile), out)
    return out


def selector(nb, sh, hw, face, side, tile_count):
    cells = side * side
    vertical = face < 2
    width = cells * tile_count if vertical else LAYERS * side * tile_count
    far_first = face in (0, 2)
    widths = by_tile(hw, tile_count, width, lambda ref, t: ref[t, face])
    slots = []
    moves = []
    for entry in range(2):
        slots.append(
            by_tile(
                nb,
                tile_count,
                width,
                lambda ref, t: jnp.where(
                    ref[t, face, entry] >= 0, lax.rem(ref[t, face, entry], tile_count), -1
                ),
            )
        )
        moves.append(by_tile(sh, tile_count, width, lambda ref, t: ref[t, face, entry]))
    col = lax.broadcasted_iota(jnp.int32, (tile_count, width), 1)

    def block(layer, position):
        keep = widths >= (LAYERS - layer if far_first else layer + 1)
        total = jnp.zeros((tile_count, width), F32)
        for slot, move in zip(slots, moves):
            along = move + position
            good = keep & (slot >= 0) & (along >= 0) & (along < side)
            if vertical:
                row = side - LAYERS + layer if far_first else layer
                target = slot * cells + row * side + along
            else:
                target = layer * (side * tile_count) + along * tile_count + slot
            total = total + jnp.where(good & (col == target), 1.0, 0.0)
        return total

    if vertical:
        blocks = [block(layer, p) for layer in range(LAYERS) for p in range(side)]
    else:
        blocks = [block(layer, p) for p in range(side) for layer in range(LAYERS)]
    return jnp.concatenate(blocks, axis=0).astype(BF16)


def edges_kernel(side, tile_count, x_ref, low_ref, high_ref):
    x = x_ref[...]
    low_ref[...] = dot(edge_order(side, tile_count, 0), x, ROWS_LANES).astype(BF16)
    high_ref[...] = dot(edge_order(side, tile_count, side - LAYERS), x, ROWS_LANES).astype(BF16)


def conv_kernel(
    side, tile_count, nb, sh, hw, x_ref, west_ref, east_ref, taps_ref, out_ref, pad_ref, tap_ref, row_ref
):
    channels = x_ref.shape[0]
    wide = side + 2 * LAYERS
    far = side + LAYERS
    tap_ref[...] = taps_ref[...].astype(F32)
    corner = jnp.zeros((LAYERS, LAYERS, tile_count, channels), F32)
    for top in (0, far):
        for left in (0, far):
            pad_ref[top : top + LAYERS, left : left + LAYERS] = corner
    x = x_ref[...]
    order = cell_order(side, tile_count)
    pad_ref[LAYERS:far, LAYERS:far] = dot(order, x, ROWS_LANES).reshape(
        side, side, tile_count, channels
    )

    def halo(face, source, dims):
        picked = dot(selector(nb, sh, hw, face, side, tile_count), source, dims)
        return picked.astype(BF16).astype(F32)

    across = (LAYERS, side, tile_count, channels)
    down = (side, LAYERS, tile_count, channels)
    plain = (((1,), (0,)), ((), ()))
    pad_ref[0:LAYERS, LAYERS:far] = halo(0, x, ROWS_LANES).reshape(across)
    pad_ref[far:wide, LAYERS:far] = halo(1, x, ROWS_LANES).reshape(across)
    pad_ref[LAYERS:far, 0:LAYERS] = halo(2, west_ref[...], plain).reshape(down)
    pad_ref[LAYERS:far, far:wide] = halo(3, east_ref[...], plain).reshape(down)

    def one_row(i, carry):
        acc = [jnp.zeros((tile_count, channels), F32) for _ in range(side)]
        for a in range(KSIZE):
            window = [pad_ref[i + a, j] for j in range(wide)]
            for b in range(KSIZE):
                tap = tap_ref[pl.ds(a * KSIZE + b, 1), :]
                for j in range(side):
                    acc[j] = acc[j] + window[j + b] * tap
        for j in range(side):
            row_ref[i, j] = acc[j]
        return carry

    lax.fori_loop(0, side, one_row, 0)
    rows = row_ref[...].reshape(side * side * tile_count, channels).astype(BF16)
    out_ref[...] = dot(rows, order, ROWS_ROWS).astype(BF16)


def back_kernel(
    side,
    tile_count,
    full_width,
    nb,
    sh,
    hw,
    p0_ref,
    p1_ref,
    p2_ref,
    p3_ref,
    conv_ref,
    stat_ref,
    gain_ref,
    taps_ref,
    out_grad_ref,
    main_ref,
    west_ref,
    east_ref,
    grad_ref,
    pad_ref,
    tap_ref,
):
    channels = conv_ref.shape[0]
    wide = side + 2 * LAYERS
    far = side + LAYERS
    tap_ref[...] = taps_ref[...].astype(F32)
    summed = (p0_ref[...].astype(F32) + p1_ref[...].astype(F32)) + (
        p2_ref[...].astype(F32) + p3_ref[...].astype(F32)
    )
    g = summed * gain_ref[...]
    mean, inv, first, second = (stat_ref[k : k + 1, :] for k in range(4))
    centered = (conv_ref[...].astype(F32) - mean) * inv
    grad_conv = (inv * (g - first / full_width - centered * (second / full_width))).astype(BF16)
    order = cell_order(side, tile_count)
    grad_ref[...] = dot(order, grad_conv, ROWS_LANES).reshape(side, side, tile_count, channels)

    def one_row(r, carry):
        def one_tap(a, acc):
            source = [grad_ref[r - a, j] for j in range(side)]
            acc = list(acc)
            for b in range(KSIZE):
                tap = tap_ref[pl.ds(a * KSIZE + b, 1), :]
                for j in range(side):
                    acc[j + b] = acc[j + b] + source[j] * tap
            return tuple(acc)

        low = jnp.maximum(r - (side - 1), 0)
        high = jnp.minimum(r, KSIZE - 1) + 1
        zero = tuple(jnp.zeros((tile_count, channels), F32) for _ in range(wide))
        acc = lax.fori_loop(low, high, one_tap, zero)
        for j in range(wide):
            pad_ref[r, j] = acc[j]
        return carry

    lax.fori_loop(0, wide, one_row, 0)

    def flat(part):
        return part.reshape(-1, channels)

    inner = flat(pad_ref[LAYERS:far, LAYERS:far])
    inner_top = inner.astype(BF16)
    inner_rest = (inner - inner_top.astype(F32)).astype(BF16)
    north = flat(pad_ref[0:LAYERS, LAYERS:far]).astype(BF16)
    south = flat(pad_ref[far:wide, LAYERS:far]).astype(BF16)
    west = flat(pad_ref[LAYERS:far, 0:LAYERS]).astype(BF16)
    east = flat(pad_ref[LAYERS:far, far:wide]).astype(BF16)
    west_ref[...] = dot(selector(nb, sh, hw, 2, side, tile_count), west, ROWS_ROWS).astype(BF16)
    east_ref[...] = dot(selector(nb, sh, hw, 3, side, tile_count), east, ROWS_ROWS).astype(BF16)
    main_ref[...] = (
        out_grad_ref[...].astype(F32)
        + dot(inner_top, order, ROWS_ROWS)
        + dot(inner_rest, order, ROWS_ROWS)
        + dot(north, selector(nb, sh, hw, 0, side, tile_count), ROWS_ROWS)
        + dot(south, selector(nb, sh, hw, 1, side, tile_count), ROWS_ROWS)
    )


def last_kernel(side, tile_count, main_ref, low_ref, high_ref, out_ref):
    total = (
        main_ref[...]
        + dot(low_ref[...], edge_order(side, tile_count, 0), ROWS_ROWS)
        + dot(high_ref[...], edge_order(side, tile_count, side - LAYERS), ROWS_ROWS)
    )
    out_ref[...] = total.astype(BF16)


def smem():
    return pl.BlockSpec(memory_space=pltpu.SMEM)


def vmem():
    return pl.BlockSpec(memory_space=pltpu.VMEM)


def flips(count, mask):
    return [(i, i ^ mask) for i in range(count)]


def pick(pair, index):
    return lax.dynamic_index_in_dim(pair, index, 0, keepdims=False)


def gather_rows(block, axis, masks):
    count = lax.axis_size(axis)
    place = lax.axis_index(axis)
    bits = count.bit_length() - 1
    held = block.reshape((1,) * bits + block.shape)
    for mask in masks:
        dim = bits - mask.bit_length()
        other = lax.ppermute(held, axis, flips(count, mask))
        upper = (place & mask) != 0
        held = jnp.where(
            upper,
            jnp.concatenate([other, held], axis=dim),
            jnp.concatenate([held, other], axis=dim),
        )
    return held.reshape((count * block.shape[0],) + block.shape[1:])


def scatter_rows(total, axis, masks):
    count = lax.axis_size(axis)
    place = lax.axis_index(axis)
    bits = count.bit_length() - 1
    held = total.reshape((2,) * bits + (total.shape[0] // count,) + total.shape[1:])
    for mask in masks:
        dim = bits - mask.bit_length()
        bit = jnp.where((place & mask) != 0, 1, 0)
        mine = lax.dynamic_slice_in_dim(held, bit, 1, axis=dim)
        theirs = lax.dynamic_slice_in_dim(held, 1 - bit, 1, axis=dim)
        other = lax.ppermute(theirs.astype(BF16), axis, flips(count, mask))
        held = mine + other.astype(F32)
    return held.reshape((total.shape[0] // count,) + total.shape[1:])


def per_device(
    tiles,
    kernel,
    norm_gain,
    w_up,
    w_down,
    layer_scale,
    neighbors,
    shifts,
    halo_widths,
    land,
    cotangent,
):
    channels = tiles.shape[0]
    tile_count, side = land.shape[0], land.shape[1]
    cells = tile_count * side * side
    edge_rows = LAYERS * side * tile_count
    wide = side + 2 * LAYERS
    parts = lax.axis_size("fsdp")
    here = lax.axis_index("fsdp")
    full_width = channels * parts
    dp = lax.axis_size("dp")
    forward = [(i, i + 1) for i in range(dp - 1)]
    backward = [(i + 1, i) for i in range(dp - 1)]
    shape = jax.ShapeDtypeStruct
    tables = (neighbors, shifts, halo_widths)
    edge = shape((edge_rows, channels), BF16)
    grid = shape((channels, cells), BF16)

    low, high = pl.pallas_call(
        lambda *refs: edges_kernel(side, tile_count, *refs),
        out_shape=(edge, edge),
        name="edges",
    )(tiles)
    west_src = lax.ppermute(high, "dp", forward)
    east_src = lax.ppermute(low, "dp", backward)

    grad_out = cotangent * land.reshape(cells)[None, :].astype(BF16)
    scale_f = layer_scale.astype(F32)[:, None]
    grad_mixed = (scale_f * grad_out.astype(F32)).astype(BF16)
    grad_mixed_all = lax.all_gather(grad_mixed, "fsdp", axis=0, tiled=True)
    gain_all = lax.all_gather(norm_gain, "fsdp", axis=0, tiled=True).astype(F32)[:, None]

    if dp & (dp - 1) == 0 and dp <= 16:
        masks = [1 << k for k in range(dp.bit_length() - 1)]
        up_full = gather_rows(w_up, "dp", masks[::-1])
        down_full = gather_rows(w_down, "dp", masks[:1] + masks[:0:-1])
    else:
        masks = None
        up_full = lax.all_gather(w_up, "dp", axis=0, tiled=True)
        down_full = lax.all_gather(w_down, "dp", axis=0, tiled=True)

    conv = pl.pallas_call(
        lambda *refs: conv_kernel(side, tile_count, *refs),
        out_shape=grid,
        in_specs=[smem()] * 3 + [vmem()] * 4,
        out_specs=vmem(),
        scratch_shapes=[
            pltpu.VMEM((wide, wide, tile_count, channels), F32),
            pltpu.VMEM(kernel.shape, F32),
            pltpu.VMEM((side, side, tile_count, channels), F32),
        ],
        name="conv",
    )(*tables, tiles, west_src, east_src, kernel)

    conv_all = lax.all_gather(conv, "fsdp", axis=0, tiled=True)
    values = lax.optimization_barrier(conv_all).astype(F32)
    mean = jnp.sum(values, axis=0) / full_width
    inv = lax.rsqrt(jnp.sum(values * values, axis=0) / full_width - mean * mean + 1e-06)
    centered = (values - mean[None, :]) * inv[None, :]
    normed = (centered * gain_all).astype(BF16)
    pre_act = dot(up_full, normed, ROWS_ROWS)
    hidden = gelu_value(pre_act).astype(BF16)
    grad_hidden = dot(down_full, grad_mixed_all, ROWS_ROWS)
    grad_pre = (grad_hidden * gelu_slope(pre_act)).astype(BF16)
    partial_grad = jnp.dot(up_full, grad_pre, preferred_element_type=F32).astype(BF16)
    weighted = partial_grad.astype(F32) * gain_all
    first, second = lax.psum(
        (jnp.sum(weighted, axis=0), jnp.sum(weighted * centered, axis=0)), "fsdp"
    )

    def exchange(partial):
        chunks = partial.reshape(parts, channels, cells)
        pieces = [pick(chunks, here)]
        for step in range(1, parts):
            ring = [(i, (i + step) % parts) for i in range(parts)]
            pieces.append(lax.ppermute(pick(chunks, (here + step) % parts), "fsdp", ring))
        return pieces

    down_local = dot(grad_mixed_all, hidden, ROWS_LANES)
    up_local = dot(normed, grad_pre, ROWS_LANES)
    pieces = exchange(partial_grad)
    stats = jnp.stack([mean, inv, first, second])
    main, to_west, to_east = pl.pallas_call(
        lambda *refs: back_kernel(side, tile_count, full_width, *refs),
        out_shape=(shape((channels, cells), F32), edge, edge),
        in_specs=[smem()] * 3 + [vmem()] * 9,
        out_specs=(vmem(),) * 3,
        scratch_shapes=[
            pltpu.VMEM((side, side, tile_count, channels), F32),
            pltpu.VMEM((wide, wide, tile_count, channels), F32),
            pltpu.VMEM(kernel.shape, F32),
        ],
        name="back",
    )(*tables, *pieces, conv, stats, norm_gain.astype(F32)[:, None], kernel, grad_out)
    from_east = lax.ppermute(to_west, "dp", backward)
    from_west = lax.ppermute(to_east, "dp", forward)
    tile_grad = pl.pallas_call(
        lambda *refs: last_kernel(side, tile_count, *refs),
        out_shape=grid,
        name="last",
    )(main, from_west, from_east)

    partial_out = jnp.dot(down_full, hidden, preferred_element_type=F32).astype(BF16)
    mixed = sum(piece.astype(F32) for piece in exchange(partial_out))
    block_out = (tiles.astype(F32) + scale_f * mixed).astype(BF16)

    if masks is not None:
        order = masks
        up_grad = scatter_rows(up_local, "dp", order)
        down_grad = scatter_rows(down_local, "dp", order)
    else:
        up_grad = lax.psum_scatter(up_local, "dp", scatter_dimension=0, tiled=True)
        down_grad = lax.psum_scatter(down_local, "dp", scatter_dimension=0, tiled=True)
    return block_out, tile_grad, up_grad, down_grad


def solution(mesh):
    return jax.shard_map(
        per_device,
        mesh=mesh,
        in_specs=(
            P("fsdp", "dp"),
            P(None, "fsdp"),
            P("fsdp"),
            P("dp", "fsdp"),
            P("dp", "fsdp"),
            P("fsdp"),
            P("dp", None, None),
            P("dp", None, None),
            P("dp", None),
            P("dp", None, None),
            P("fsdp", "dp"),
        ),
        out_specs=(P("fsdp", "dp"), P("fsdp", "dp"), P("dp", "fsdp"), P("dp", "fsdp")),
        check_vma=False,
    )
```
